1024 devices in a mesh: section: 4 (over x_lo, core), dp: 16 (over x_hi, y), tensor: 16 (over z).
Axes of the slice: x: 4 (x_hi: 2, x_lo: 2; x = x_hi * 2 + x_lo), y: 8, z: 16, core: 2. Of those that a mesh axis runs over, the one named last changes fastest.
Arguments:
- image_tokens: bfloat16 [16, 512, 8192], P('dp', 'section', 'tensor'), may hold values from -6 to 6
- kv_weight: bfloat16 [4, 8192, 1024], P('section', 'tensor'), may hold values from -0.0625 to 0.0625
- queries: bfloat16 [4, 16, 256, 8192], P('section', 'dp', None, 'tensor'), may hold values from -400 to 400
- out_weight: bfloat16 [4, 8192, 8192], P('section', 'tensor'), may hold values from -0.0625 to 0.0625
- residual: bfloat16 [4, 16, 256, 8192], P('section', 'dp', 'tensor'), may hold values from -1.796875 to 1.796875
- gate: float32 [4], P('section'), may hold values from 0.3 to 1.5
- tile_counts: int32 [16], P('dp'), may hold values from 1 to 4, as said below
Outputs:
- mixed: bfloat16 [4, 16, 256, 8192], P('section', 'dp', 'tensor')
The draws below stay inside these ranges and needn't reach their ends.
Inputs may be any that keep to these rules, and one draw needn't show every extreme that they name: `tile_counts`: every sample has at least one tile, and some sample has all 4.
All inputs are finite; a program needn't handle non-finite values.
Results may differ from the reference program's by a relative error of at most 0.019.
Values may be sent and summed in bfloat16 or wider, within the bound.
No kernel may reach another device: no remote copies, remote signals or barrier semaphores. Data moves between devices by JAX's collectives and lax.ppermute only.
A program may use at most 32 MiB of HBM per device.

```python
import math
import jax
import jax.numpy as jnp
from jax import lax

D = 8192
HD = 128
QH = 64
KVH = 4
TILES = 4
TILE_ROWS = 128
TXT = 256
IMG = 512
KVW = 512
SAMPLES = 16
N_SECTION = 4
N_TENSOR = 16


def draw_queries(key, part):
    full_shape = (N_SECTION, SAMPLES, TXT, QH * HD)
    normal_draw = jax.random.normal(jax.random.fold_in(key, 11), full_shape, jnp.float32)
    return (jnp.clip(normal_draw, -6.0, 6.0) * 1.5).astype(jnp.bfloat16)


def draw_tile_counts(key, part):
    counts = jax.random.randint(jax.random.fold_in(key, 21), (SAMPLES,), 1, TILES + 1)
    chosen = jax.random.randint(jax.random.fold_in(key, 22), (), 0, SAMPLES)
    return jnp.where(jnp.arange(SAMPLES) == chosen, TILES, counts).astype(jnp.int32)


def block_scale(key, extent, shards, low, largest):
    gain, own = 1.0, jax.random.fold_in(key, 6)
    for position, parts in shards:
        draws = jnp.exp(jax.random.uniform(jax.random.fold_in(own, position), (parts,), jnp.float32, low / len(shards), largest / len(shards)))
        gain = gain * jnp.repeat(draws, extent[position] // parts).reshape([-1 if axis == position else 1 for axis in range(len(extent))])
    return gain


def noise(rng, shape, spread, limit, cuts=(), held_as=jnp.bfloat16):
    values = jax.random.normal(rng, shape, jnp.float32) * spread
    if len(cuts) > 0:
        values = block_scale(rng, shape, cuts, -0.22, 0.18) * values
    return jnp.clip(values, min=-limit, max=limit).astype(held_as)


def setup_inputs(seed: int = 0) -> dict:
    streams_of = jax.random.split(jax.random.key(seed), 8)
    return {
        "image_tokens": noise(streams_of[0], (SAMPLES, IMG, D), 1.0, 6.0, ((0, 16), (1, 4), (2, 16))),
        "kv_weight": noise(streams_of[1], (N_SECTION, D, 2 * KVW), D ** -0.5, 0.0625, ((0, 4), (1, 16))),
        "queries": draw_queries(jax.random.fold_in(streams_of[7], 71), 0),
        "out_weight": noise(streams_of[3], (N_SECTION, QH * HD, D), (QH * HD) ** -0.5, 0.0625, ((0, 4), (1, 16))),
        "residual": noise(streams_of[4], (N_SECTION, SAMPLES, TXT, D), 0.3, 1.796875, ((0, 4), (1, 16), (2, 16))),
        "gate": jnp.clip(0.3 + 1.2 * jax.random.uniform(streams_of[5], (N_SECTION,), jnp.float32) ** block_scale(streams_of[5], (N_SECTION,), ((0, 4),), -0.2, 0.2), 0.3, 1.5),
        "tile_counts": draw_tile_counts(jax.random.fold_in(streams_of[7], 71), 0),
    }


def reference(image_tokens, kv_weight, queries, out_weight, residual, gate, tile_counts):
    group_size = QH // KVH
    column_band = QH // N_TENSOR * HD
    key_tile = jnp.arange(IMG, dtype=jnp.int32) // TILE_ROWS
    results = []
    for section_index in range(N_SECTION):
        pair_weight = kv_weight[section_index]
        proj_weight = out_weight[section_index]
        gate_scale = jnp.tanh(gate[section_index])

        def one_sample(inputs_one):
            image_one, question, residual_one, tile_count = inputs_one
            keys_values = jnp.dot(image_one, pair_weight, preferred_element_type=jnp.float32).astype(jnp.bfloat16)
            visible = key_tile < tile_count
            head_outputs = []
            for head_index in range(QH):
                group_index = head_index // group_size
                key_block = keys_values[:, group_index * HD:(group_index + 1) * HD]
                value_block = keys_values[:, KVW + group_index * HD:KVW + (group_index + 1) * HD]
                query_block = question[:, head_index * HD:(head_index + 1) * HD]
                logits = jnp.dot(query_block, key_block.T, preferred_element_type=jnp.float32) / math.sqrt(HD)
                logits = jnp.where(visible[None, :], logits, -jnp.inf)
                weights = jax.nn.softmax(logits, axis=-1).astype(jnp.bfloat16)
                head_outputs.append(jnp.dot(weights, value_block, preferred_element_type=jnp.float32).astype(jnp.bfloat16))
            attended = jnp.concatenate(head_outputs, axis=1)
            summed = jnp.zeros((TXT, D), jnp.float32)
            for band_index in range(N_TENSOR):
                lower = band_index * column_band
                partial_value = jnp.dot(attended[:, lower:lower + column_band], proj_weight[lower:lower + column_band], preferred_element_type=jnp.float32)
                summed = summed + partial_value.astype(jnp.bfloat16).astype(jnp.float32)
            return (residual_one.astype(jnp.float32) + gate_scale * summed).astype(jnp.bfloat16)
        results.append(lax.map(one_sample, (image_tokens, queries[section_index], residual[section_index], tile_counts)))
    return jnp.stack(results)
```

```python
import functools
import math

import jax
import jax.numpy as jnp
from jax import lax
from jax.experimental import pallas as pl
from jax.experimental.pallas import tpu as pltpu
from jax.sharding import PartitionSpec as P

HD = 128
KVH = 4
TILE_ROWS = 128
NT = 16
QUAD = NT // KVH

VMEM = pl.BlockSpec(memory_space=pltpu.VMEM)
SMEM = pl.BlockSpec(memory_space=pltpu.SMEM)


def hop(x, by):
    return lax.ppermute(x, "tensor", [(i, (i + by) % NT) for i in range(NT)])


def quad_hop(x, by):
    return lax.ppermute(
        x, "tensor", [(i, i // QUAD * QUAD + (i % QUAD + by) % QUAD) for i in range(NT)]
    )


def kv_kernel(x_ref, w_ref, o_ref):
    x = x_ref[...]
    for c in range(KVH):
        p = jnp.dot(x, w_ref[:, c * 256 : (c + 1) * 256], preferred_element_type=jnp.float32)
        for half in range(2):
            o_ref[2 * c + half] = p[:, half * HD : (half + 1) * HD]


def kv_partial(x, w):
    return pl.pallas_call(
        kv_kernel,
        out_shape=jax.ShapeDtypeStruct((2 * KVH, x.shape[0], HD), jnp.float32),
        in_specs=[VMEM, VMEM],
        out_specs=VMEM,
        compiler_params=pltpu.CompilerParams(vmem_limit_bytes=16 << 20),
        name="kv_partial",
    )(x, w)


def attention_kernel(valid_ref, q_ref, kv0_ref, kv1_ref, kv2_ref, kv3_ref, o_ref):
    blocks = (kv0_ref, kv1_ref, kv2_ref, kv3_ref)
    keys = jnp.concatenate([b[0] for b in blocks], axis=0)
    values = jnp.concatenate([b[1] for b in blocks], axis=0)
    bias = jnp.concatenate(
        [
            jnp.full((1, TILE_ROWS), jnp.where(valid_ref[i] > 0, 0.0, -jnp.inf), jnp.float32)
            for i in range(len(blocks))
        ],
        axis=1,
    )
    for h in range(q_ref.shape[1] // HD):
        q = q_ref[:, h * HD : (h + 1) * HD]
        s = lax.dot_general(
            q, keys, (((1,), (1,)), ((), ())), preferred_element_type=jnp.float32
        )
        s = s * (1.0 / math.sqrt(HD)) + bias
        e = jnp.exp(s - jnp.max(s, axis=1, keepdims=True))
        p = (e / jnp.sum(e, axis=1, keepdims=True)).astype(jnp.bfloat16)
        o_ref[:, h * HD : (h + 1) * HD] = jnp.dot(
            p, values, preferred_element_type=jnp.float32
        ).astype(jnp.bfloat16)


def attention(valid, q, blocks):
    return pl.pallas_call(
        attention_kernel,
        out_shape=jax.ShapeDtypeStruct(q.shape, jnp.bfloat16),
        in_specs=[SMEM] + [VMEM] * 5,
        out_specs=VMEM,
        compiler_params=pltpu.CompilerParams(vmem_limit_bytes=16 << 20),
        name="attention",
    )(valid, q, *blocks)


def add16(a, b):
    return (a.astype(jnp.float32) + b.astype(jnp.float32)).astype(jnp.bfloat16)


def local(image_tokens, kv_weight, queries, out_weight, residual, gate, tile_counts):
    me = lax.axis_index("tensor")
    member = me % QUAD
    rows = queries.shape[2] // NT
    q = queries[0, 0]
    q = lax.dynamic_slice_in_dim(jnp.concatenate([q, q], axis=0), me * rows, NT * rows, 0)

    tokens = lax.all_gather(image_tokens[0], "section", axis=0, tiled=True)
    partial = kv_partial(tokens, kv_weight[0]).reshape(2, NT, TILE_ROWS, HD)

    def mine(owner):
        return lax.dynamic_slice_in_dim(partial, owner % NT, 1, 1)[:, 0]

    up, down = mine(me + 8), mine(me + 9)
    for k in range(1, 9):
        up = hop(up, 1)
        if k < 8:
            down = hop(down, -1)
        if k < 8:
            up = up + mine(me + 8 - k + NT)
        if k < 7:
            down = down + mine(me + 9 + k)
    own = (up + down + mine(me)).astype(jnp.bfloat16)
    blocks = [own] + [quad_hop(own, k) for k in range(1, QUAD)]
    tiles = (member - jnp.arange(QUAD, dtype=jnp.int32)) % QUAD
    valid = (tiles < tile_counts[0]).astype(jnp.int32)
    attended = attention(valid, q, blocks)

    weight = out_weight[0]

    def project(first, last):
        part = jnp.dot(
            attended[first * rows : last * rows], weight, preferred_element_type=jnp.float32
        ).astype(jnp.bfloat16)
        return {p: part[(p - first) * rows : (p - first + 1) * rows] for p in range(first, last)}

    parts = {**project(6, 12), **project(12, 16), **project(0, 6)}
    up, down = parts[8], parts[9]
    for k in range(1, 9):
        up = hop(up, 1)
        if k < 8:
            down = hop(down, -1)
        if k < 8:
            up = add16(up, parts[8 - k])
        if k < 7:
            down = add16(down, parts[9 + k])
    total = up.astype(jnp.float32) + down.astype(jnp.float32) + parts[0].astype(jnp.float32)
    mixed = (residual[0, 0].astype(jnp.float32) + jnp.tanh(gate[0]) * total).astype(jnp.bfloat16)
    return mixed[None, None]


def solution(mesh):
    return jax.shard_map(
        local,
        mesh=mesh,
        in_specs=(
            P("dp", "section", "tensor"),
            P("section", "tensor", None),
            P("section", "dp", None, "tensor"),
            P("section", "tensor", None),
            P("section", "dp", "tensor", None),
            P("section"),
            P("dp"),
        ),
        out_specs=P("section", "dp", "tensor", None),
        check_vma=False,
    )
```

```python
import functools
import math

import jax
import jax.numpy as jnp
from jax import lax
from jax.experimental import pallas as pl
from jax.experimental.pallas import tpu as pltpu
from jax.sharding import PartitionSpec as P

HD = 128
KVH = 4
TILE_ROWS = 128
NT = 16
NS = 4
QUAD = NT // KVH

VMEM = pl.BlockSpec(memory_space=pltpu.VMEM)
SMEM = pl.BlockSpec(memory_space=pltpu.SMEM)


def both_ways(step):
    pairs = []
    for section in range(NS):
        way = 1 - 2 * (section % 2)
        pairs += [(section * NT + i, section * NT + step(i, way)) for i in range(NT)]
    return pairs


def hop(x, by):
    return lax.ppermute(x, ("section", "tensor"), both_ways(lambda i, way: (i + way * by) % NT))


def quad_hop(x, by):
    return lax.ppermute(
        x,
        ("section", "tensor"),
        both_ways(lambda i, way: i // QUAD * QUAD + (i % QUAD + way * by) % QUAD),
    )


def kv_kernel(x_ref, w_ref, o_ref):
    x = x_ref[...]
    for c in range(KVH):
        p = jnp.dot(x, w_ref[:, c * 256 : (c + 1) * 256], preferred_element_type=jnp.float32)
        for half in range(2):
            o_ref[2 * c + half] = p[:, half * HD : (half + 1) * HD]


def kv_partial(x, w):
    return pl.pallas_call(
        kv_kernel,
        out_shape=jax.ShapeDtypeStruct((2 * KVH, x.shape[0], HD), jnp.float32),
        in_specs=[VMEM, VMEM],
        out_specs=VMEM,
        compiler_params=pltpu.CompilerParams(vmem_limit_bytes=16 << 20),
        name="kv_partial",
    )(x, w)


def add_block_kernel(index_ref, sum_ref, partial_ref, o_ref):
    o_ref[...] = sum_ref[...] + partial_ref[:, index_ref[0]]


def add_block(total, partial, index):
    return pl.pallas_call(
        add_block_kernel,
        out_shape=jax.ShapeDtypeStruct(total.shape, total.dtype),
        in_specs=[SMEM, VMEM, VMEM],
        out_specs=VMEM,
        compiler_params=pltpu.CompilerParams(vmem_limit_bytes=8 << 20),
        name="add_block",
    )(index.reshape(1), total, partial)


def attend_kernel(
    valid_ref, order_ref, q_ref, kv0_ref, kv1_ref, kv2_ref, kv3_ref, w_ref, o_ref,
    q_scr, att_scr, w_scr, sems,
):
    pieces, _, width = w_scr.shape

    def fetch(i):
        columns = pl.ds(pl.multiple_of(i * width, width), width)
        return pltpu.make_async_copy(w_ref.at[:, columns], w_scr.at[i], sems.at[i])

    for i in range(pieces):
        fetch(i).start()

    rows = q_scr.shape[0] // NT
    for p in range(NT):
        start = pl.multiple_of(order_ref[p] * rows, rows)
        q_scr[p * rows : (p + 1) * rows, :] = q_ref[pl.ds(start, rows), :]
    blocks = (kv0_ref, kv1_ref, kv2_ref, kv3_ref)
    keys = jnp.concatenate([b[0] for b in blocks], axis=0)
    values = jnp.concatenate([b[1] for b in blocks], axis=0)
    bias = jnp.concatenate(
        [
            jnp.full((1, TILE_ROWS), jnp.where(valid_ref[i] > 0, 0.0, -jnp.inf), jnp.float32)
            for i in range(len(blocks))
        ],
        axis=1,
    )
    for h in range(q_scr.shape[1] // HD):
        q = q_scr[:, h * HD : (h + 1) * HD]
        s = lax.dot_general(
            q, keys, (((1,), (1,)), ((), ())), preferred_element_type=jnp.float32
        )
        s = s * (1.0 / math.sqrt(HD)) + bias
        e = jnp.exp(s - jnp.max(s, axis=1, keepdims=True))
        p = (e / jnp.sum(e, axis=1, keepdims=True)).astype(jnp.bfloat16)
        att_scr[:, h * HD : (h + 1) * HD] = jnp.dot(
            p, values, preferred_element_type=jnp.float32
        ).astype(jnp.bfloat16)

    @pl.loop(0, pieces)
    def _(i):
        fetch(i).wait()
        columns = pl.ds(pl.multiple_of(i * width, width), width)
        o_ref[:, columns] = jnp.dot(
            att_scr[...], w_scr[i], preferred_element_type=jnp.float32
        ).astype(jnp.bfloat16)


def attend_and_project(valid, order, q, blocks, weight):
    depth, columns = weight.shape
    width = 1024
    pieces = columns // width
    return pl.pallas_call(
        attend_kernel,
        out_shape=jax.ShapeDtypeStruct((q.shape[0], columns), jnp.bfloat16),
        in_specs=[SMEM, SMEM] + [VMEM] * 5 + [pl.BlockSpec(memory_space=pltpu.HBM)],
        out_specs=VMEM,
        scratch_shapes=[
            pltpu.VMEM(q.shape, jnp.bfloat16),
            pltpu.VMEM(q.shape, jnp.bfloat16),
            pltpu.VMEM((pieces, depth, width), jnp.bfloat16),
            pltpu.SemaphoreType.DMA((pieces,)),
        ],
        compiler_params=pltpu.CompilerParams(vmem_limit_bytes=44 << 20),
        name="attend_and_project",
    )(valid, order, q, *blocks, weight)


def add_rows_kernel(first, sum_ref, part_ref, o_ref):
    rows = sum_ref.shape[0]
    o_ref[...] = (
        sum_ref[...].astype(jnp.float32) + part_ref[first : first + rows, :].astype(jnp.float32)
    ).astype(jnp.bfloat16)


def add_rows(total, projected, block):
    return pl.pallas_call(
        functools.partial(add_rows_kernel, block * total.shape[0]),
        out_shape=jax.ShapeDtypeStruct(total.shape, total.dtype),
        in_specs=[VMEM, VMEM],
        out_specs=VMEM,
        compiler_params=pltpu.CompilerParams(vmem_limit_bytes=8 << 20),
        name="add_rows",
    )(total, projected)


def local(image_tokens, kv_weight, queries, out_weight, residual, gate, tile_counts):
    me = lax.axis_index("tensor")
    way = 1 - 2 * (lax.axis_index("section") % 2)
    member = me % QUAD
    order = (me + way * jnp.arange(NT, dtype=jnp.int32)) % NT
    rows = queries.shape[2] // NT

    tokens = lax.all_gather(image_tokens[0], "section", axis=0, tiled=True)
    partial = kv_partial(tokens, kv_weight[0]).reshape(2, NT, TILE_ROWS, HD)

    up = lax.dynamic_slice_in_dim(partial, order[8], 1, 1)[:, 0]
    down = lax.dynamic_slice_in_dim(partial, order[9], 1, 1)[:, 0]
    for k in range(1, 9):
        up = hop(up, 1)
        if k < 8:
            down = hop(down, -1)
            up = add_block(up, partial, order[8 - k])
        if k < 7:
            down = add_block(down, partial, order[9 + k])
    own = (up + down + lax.dynamic_slice_in_dim(partial, me, 1, 1)[:, 0]).astype(jnp.bfloat16)
    blocks = [own] + [quad_hop(own, k) for k in range(1, QUAD)]
    tiles = (member - way * jnp.arange(QUAD, dtype=jnp.int32)) % QUAD
    valid = (tiles < tile_counts[0]).astype(jnp.int32)
    projected = attend_and_project(valid, order, queries[0, 0], blocks, out_weight[0])

    def part(p):
        return projected[p * rows : (p + 1) * rows]

    up, down = part(8), part(9)
    for k in range(1, 9):
        up = hop(up, 1)
        if k < 8:
            down = hop(down, -1)
            up = add_rows(up, projected, 8 - k)
        if k < 7:
            down = add_rows(down, projected, 9 + k)
    total = up.astype(jnp.float32) + down.astype(jnp.float32) + part(0).astype(jnp.float32)
    mixed = (residual[0, 0].astype(jnp.float32) + jnp.tanh(gate[0]) * total).astype(jnp.bfloat16)
    return mixed[None, None]


def solution(mesh):
    return jax.shard_map(
        local,
        mesh=mesh,
        in_specs=(
            P("dp", "section", "tensor"),
            P("section", "tensor", None),
            P("section", "dp", None, "tensor"),
            P("section", "tensor", None),
            P("section", "dp", "tensor", None),
            P("section"),
            P("dp"),
        ),
        out_specs=P("section", "dp", "tensor", None),
        check_vma=False,
    )
```

```python
import functools
import math

import jax
import jax.numpy as jnp
from jax import lax
from jax.experimental import pallas as pl
from jax.experimental.pallas import tpu as pltpu
from jax.sharding import PartitionSpec as P

HD = 128
KVH = 4
TILE_ROWS = 128
NT = 16
NS = 4
HALVES = 2
QUAD = NT // KVH

VMEM = pl.BlockSpec(memory_space=pltpu.VMEM)
SMEM = pl.BlockSpec(memory_space=pltpu.SMEM)


def hop(x, by):
    pairs = []
    for section in range(NS):
        way = 1 - 2 * (section % 2)
        pairs += [(section * NT + i, section * NT + (i + way * by) % NT) for i in range(NT)]
    return lax.ppermute(x, ("section", "tensor"), pairs)


def swap(x, bit):
    return lax.ppermute(x, "tensor", [(i, i ^ bit) for i in range(NT)])


def kv_kernel(order_ref, x_ref, w_ref, o_ref, scr):
    x = x_ref[...]
    for c in range(KVH):
        p = jnp.dot(x, w_ref[:, c * 256 : (c + 1) * 256], preferred_element_type=jnp.float32)
        for half in range(2):
            for r in range(QUAD):
                scr[(2 * c + half) * QUAD + r] = p[
                    r * TILE_ROWS : (r + 1) * TILE_ROWS, half * HD : (half + 1) * HD
                ]
    for p in range(NT):
        o_ref[p, 0] = scr[order_ref[p]]
        o_ref[p, 1] = scr[NT + order_ref[p]]


def kv_partial(order, x, w):
    return pl.pallas_call(
        kv_kernel,
        out_shape=jax.ShapeDtypeStruct((NT, 2, TILE_ROWS, HD), jnp.float32),
        in_specs=[SMEM, VMEM, VMEM],
        out_specs=VMEM,
        scratch_shapes=[pltpu.VMEM((2 * NT, TILE_ROWS, HD), jnp.float32)],
        compiler_params=pltpu.CompilerParams(vmem_limit_bytes=16 << 20),
        name="kv_partial",
    )(order, x, w)


def add_block_kernel(block, sum_ref, partial_ref, o_ref):
    o_ref[...] = sum_ref[...] + partial_ref[block]


def add_block(total, partial, block):
    return pl.pallas_call(
        functools.partial(add_block_kernel, block),
        out_shape=jax.ShapeDtypeStruct(total.shape, total.dtype),
        in_specs=[VMEM, VMEM],
        out_specs=VMEM,
        compiler_params=pltpu.CompilerParams(vmem_limit_bytes=8 << 20),
        name="add_block",
    )(total, partial)


def attend_kernel(
    valid_ref, order_ref, q_ref, near_ref, far_ref, w_ref, o_ref, q_scr, att_scr, w_scr, sems,
):
    pieces, _, width = w_scr.shape

    def fetch(i):
        columns = pl.ds(pl.multiple_of(i * width, width), width)
        return pltpu.make_async_copy(w_ref.at[:, columns], w_scr.at[i], sems.at[i])

    for i in range(pieces):
        fetch(i).start()

    rows = q_scr.shape[0] // NT
    for p in range(NT):
        start = pl.multiple_of(order_ref[p] * rows, rows)
        q_scr[p * rows : (p + 1) * rows, :] = q_ref[pl.ds(start, rows), :]
    blocks = [pair[i] for pair in (near_ref, far_ref) for i in range(2)]
    keys = jnp.concatenate([b[0] for b in blocks], axis=0)
    values = jnp.concatenate([b[1] for b in blocks], axis=0)
    bias = jnp.concatenate(
        [
            jnp.full((1, TILE_ROWS), jnp.where(valid_ref[i] > 0, 0.0, -jnp.inf), jnp.float32)
            for i in range(len(blocks))
        ],
        axis=1,
    )
    for h in range(q_scr.shape[1] // HD):
        q = q_scr[:, h * HD : (h + 1) * HD]
        s = lax.dot_general(
            q, keys, (((1,), (1,)), ((), ())), preferred_element_type=jnp.float32
        )
        s = s * (1.0 / math.sqrt(HD)) + bias
        e = jnp.exp(s - jnp.max(s, axis=1, keepdims=True))
        p = (e / jnp.sum(e, axis=1, keepdims=True)).astype(jnp.bfloat16)
        att_scr[:, h * HD : (h + 1) * HD] = jnp.dot(
            p, values, preferred_element_type=jnp.float32
        ).astype(jnp.bfloat16)

    @pl.loop(0, pieces)
    def _(i):
        fetch(i).wait()
        columns = pl.ds(pl.multiple_of(i * width, width), width)
        o_ref[:, columns] = jnp.dot(
            att_scr[...], w_scr[i], preferred_element_type=jnp.float32
        ).astype(jnp.bfloat16)


def attend_and_project(valid, order, q, near, far, weight):
    depth, columns = weight.shape
    width = 1024
    pieces = columns // width
    return pl.pallas_call(
        attend_kernel,
        out_shape=jax.ShapeDtypeStruct((q.shape[0], columns), jnp.bfloat16),
        in_specs=[SMEM, SMEM] + [VMEM] * 3 + [pl.BlockSpec(memory_space=pltpu.HBM)],
        out_specs=VMEM,
        scratch_shapes=[
            pltpu.VMEM(q.shape, jnp.bfloat16),
            pltpu.VMEM(q.shape, jnp.bfloat16),
            pltpu.VMEM((pieces, depth, width), jnp.bfloat16),
            pltpu.SemaphoreType.DMA((pieces,)),
        ],
        compiler_params=pltpu.CompilerParams(vmem_limit_bytes=44 << 20),
        name="attend_and_project",
    )(valid, order, q, near, far, weight)


def add_rows_kernel(block, half, sum_ref, part_ref, o_ref):
    rows, columns = sum_ref.shape
    part = part_ref[block * rows : (block + 1) * rows, half * columns : (half + 1) * columns]
    o_ref[...] = (sum_ref[...].astype(jnp.float32) + part.astype(jnp.float32)).astype(jnp.bfloat16)


def add_rows(total, projected, block, half):
    return pl.pallas_call(
        functools.partial(add_rows_kernel, block, half),
        out_shape=jax.ShapeDtypeStruct(total.shape, total.dtype),
        in_specs=[VMEM, VMEM],
        out_specs=VMEM,
        compiler_params=pltpu.CompilerParams(vmem_limit_bytes=8 << 20),
        name="add_rows",
    )(total, projected)


def local(image_tokens, kv_weight, queries, out_weight, residual, gate, tile_counts):
    me = lax.axis_index("tensor")
    way = 1 - 2 * (lax.axis_index("section") % 2)
    member = me % QUAD
    order = (me + way * jnp.arange(NT, dtype=jnp.int32)) % NT
    rows = queries.shape[2] // NT

    tokens = lax.all_gather(image_tokens[0], "section", axis=0, tiled=True)
    partial = kv_partial(order, tokens, kv_weight[0])
    chains = (
        (8, ((2, 6), (2, 4), (2, 2), (2, None))),
        (9, ((-2, 11), (-2, 13), (-2, 15), (-1, None))),
        (7, ((2, 5), (2, 3), (2, 1), (1, None))),
        (10, ((-2, 12), (-2, 14), (-2, None))),
    )
    sums = [partial[first] for first, _ in chains]
    for k in range(4):
        for c, (_, steps) in enumerate(chains):
            if k < len(steps):
                by, block = steps[k]
                sums[c] = hop(sums[c], by)
                if block is not None:
                    sums[c] = add_block(sums[c], partial, block)
    own = (partial[0] + sums[0] + sums[1] + sums[2] + sums[3]).astype(jnp.bfloat16)
    near = jnp.stack([own, swap(own, 1)])
    far = swap(near, 2)
    tiles = member ^ jnp.arange(QUAD, dtype=jnp.int32)
    valid = (tiles < tile_counts[0]).astype(jnp.int32)
    projected = attend_and_project(valid, order, queries[0, 0], near, far, out_weight[0])

    width = projected.shape[1] // HALVES

    def part(p, half):
        return projected[p * rows : (p + 1) * rows, half * width : (half + 1) * width]

    ups = [part(8, half) for half in range(HALVES)]
    downs = [part(9, half) for half in range(HALVES)]
    for k in range(1, 9):
        for half in range(HALVES):
            ups[half] = hop(ups[half], 1)
            if k < 8:
                downs[half] = hop(downs[half], -1)
                ups[half] = add_rows(ups[half], projected, 8 - k, half)
            if k < 7:
                downs[half] = add_rows(downs[half], projected, 9 + k, half)
    total = jnp.concatenate(
        [
            ups[half].astype(jnp.float32)
            + downs[half].astype(jnp.float32)
            + part(0, half).astype(jnp.float32)
            for half in range(HALVES)
        ],
        axis=1,
    )
    mixed = (residual[0, 0].astype(jnp.float32) + jnp.tanh(gate[0]) * total).astype(jnp.bfloat16)
    return mixed[None, None]


def solution(mesh):
    return jax.shard_map(
        local,
        mesh=mesh,
        in_specs=(
            P("dp", "section", "tensor"),
            P("section", "tensor", None),
            P("section", "dp", None, "tensor"),
            P("section", "tensor", None),
            P("section", "dp", "tensor", None),
            P("section"),
            P("dp"),
        ),
        out_specs=P("section", "dp", "tensor", None),
        check_vma=False,
    )
```

```python
import functools
import math

import jax
import jax.numpy as jnp
from jax import lax
from jax.experimental import pallas as pl
from jax.experimental.pallas import tpu as pltpu
from jax.sharding import PartitionSpec as P

HD = 128
KVH = 4
TILE_ROWS = 128
NT = 16
NS = 4
QUAD = NT // KVH

VMEM = pl.BlockSpec(memory_space=pltpu.VMEM)
SMEM = pl.BlockSpec(memory_space=pltpu.SMEM)


def both_ways(step):
    pairs = []
    for section in range(NS):
        way = 1 - 2 * (section % 2)
        pairs += [(section * NT + i, section * NT + step(i, way)) for i in range(NT)]
    return pairs


def hop(x, by):
    return lax.ppermute(x, ("section", "tensor"), both_ways(lambda i, way: (i + way * by) % NT))


def attend_kernel(index_ref, q_ref, kv_ref, w_ref, o_ref, q_scr, att_scr, w_scr, sems):
    pieces, _, width = w_scr.shape

    def fetch(i):
        columns = pl.ds(pl.multiple_of(i * width, width), width)
        return pltpu.make_async_copy(w_ref.at[:, columns], w_scr.at[i], sems.at[i])

    for i in range(pieces):
        fetch(i).start()

    rows = q_scr.shape[0] // NT
    for p in range(NT):
        start = pl.multiple_of(index_ref[p] * rows, rows)
        q_scr[p * rows : (p + 1) * rows, :] = q_ref[pl.ds(start, rows), :]
    group = index_ref[NT]
    keys = kv_ref[:, pl.ds(pl.multiple_of(group * HD, HD), HD)]
    values = kv_ref[:, pl.ds(pl.multiple_of((KVH + group) * HD, HD), HD)]
    bias = jnp.concatenate(
        [
            jnp.full((1, TILE_ROWS), jnp.where(i < index_ref[NT + 1], 0.0, -jnp.inf), jnp.float32)
            for i in range(kv_ref.shape[0] // TILE_ROWS)
        ],
        axis=1,
    )
    for h in range(q_scr.shape[1] // HD):
        q = q_scr[:, h * HD : (h + 1) * HD]
        s = lax.dot_general(
            q, keys, (((1,), (1,)), ((), ())), preferred_element_type=jnp.float32
        )
        s = s * (1.0 / math.sqrt(HD)) + bias
        e = jnp.exp(s - jnp.max(s, axis=1, keepdims=True))
        p = (e / jnp.sum(e, axis=1, keepdims=True)).astype(jnp.bfloat16)
        att_scr[:, h * HD : (h + 1) * HD] = jnp.dot(
            p, values, preferred_element_type=jnp.float32
        ).astype(jnp.bfloat16)

    @pl.loop(0, pieces)
    def _(i):
        fetch(i).wait()
        columns = pl.ds(pl.multiple_of(i * width, width), width)
        o_ref[:, columns] = jnp.dot(
            att_scr[...], w_scr[i], preferred_element_type=jnp.float32
        ).astype(jnp.bfloat16)


def attend_and_project(index, q, kv, weight):
    depth, columns = weight.shape
    width = 1024
    pieces = columns // width
    return pl.pallas_call(
        attend_kernel,
        out_shape=jax.ShapeDtypeStruct((q.shape[0], columns), jnp.bfloat16),
        in_specs=[SMEM, VMEM, VMEM] + [pl.BlockSpec(memory_space=pltpu.HBM)],
        out_specs=VMEM,
        scratch_shapes=[
            pltpu.VMEM(q.shape, jnp.bfloat16),
            pltpu.VMEM(q.shape, jnp.bfloat16),
            pltpu.VMEM((pieces, depth, width), jnp.bfloat16),
            pltpu.SemaphoreType.DMA((pieces,)),
        ],
        compiler_params=pltpu.CompilerParams(vmem_limit_bytes=44 << 20),
        name="attend_and_project",
    )(index, q, kv, weight)


def add_rows_kernel(first, sum_ref, part_ref, o_ref):
    rows = sum_ref.shape[0]
    o_ref[...] = (
        sum_ref[...].astype(jnp.float32) + part_ref[first : first + rows, :].astype(jnp.float32)
    ).astype(jnp.bfloat16)


def add_rows(total, projected, block):
    return pl.pallas_call(
        functools.partial(add_rows_kernel, block * total.shape[0]),
        out_shape=jax.ShapeDtypeStruct(total.shape, total.dtype),
        in_specs=[VMEM, VMEM],
        out_specs=VMEM,
        compiler_params=pltpu.CompilerParams(vmem_limit_bytes=8 << 20),
        name="add_rows",
    )(total, projected)


def local(image_tokens, kv_weight, queries, out_weight, residual, gate, tile_counts):
    me = lax.axis_index("tensor")
    way = 1 - 2 * (lax.axis_index("section") % 2)
    order = (me + way * jnp.arange(NT, dtype=jnp.int32)) % NT
    rows = queries.shape[2] // NT

    tokens = lax.all_gather(image_tokens[0], "section", axis=0, tiled=True)
    partial = jnp.dot(tokens, kv_weight[0], preferred_element_type=jnp.float32)
    keys_values = lax.psum(partial, "tensor").astype(jnp.bfloat16)
    index = jnp.concatenate([order, (me // QUAD).reshape(1), tile_counts])
    projected = attend_and_project(index, queries[0, 0], keys_values, out_weight[0])

    def part(p):
        return projected[p * rows : (p + 1) * rows]

    up, down = part(8), part(9)
    for k in range(1, 9):
        up = hop(up, 1)
        if k < 8:
            down = hop(down, -1)
            up = add_rows(up, projected, 8 - k)
        if k < 7:
            down = add_rows(down, projected, 9 + k)
    total = up.astype(jnp.float32) + down.astype(jnp.float32) + part(0).astype(jnp.float32)
    mixed = (residual[0, 0].astype(jnp.float32) + jnp.tanh(gate[0]) * total).astype(jnp.bfloat16)
    return mixed[None, None]


def solution(mesh):
    return jax.shard_map(
        local,
        mesh=mesh,
        in_specs=(
            P("dp", "section", "tensor"),
            P("section", "tensor", None),
            P("section", "dp", None, "tensor"),
            P("section", "tensor", None),
            P("section", "dp", "tensor", None),
            P("section"),
            P("dp"),
        ),
        out_specs=P("section", "dp", "tensor", None),
        check_vma=False,
    )
```

```python
import functools
import math

import jax
import jax.numpy as jnp
from jax import lax
from jax.experimental import pallas as pl
from jax.experimental.pallas import tpu as pltpu
from jax.sharding import PartitionSpec as P

HD = 128
KVH = 4
TILE_ROWS = 128
NT = 16
NS = 4
QUAD = NT // KVH

VMEM = pl.BlockSpec(memory_space=pltpu.VMEM)


def both_ways(step):
    pairs = []
    for section in range(NS):
        way = 1 - 2 * (section % 2)
        pairs += [(section * NT + i, section * NT + step(i, way)) for i in range(NT)]
    return pairs


def hop(x, by):
    return lax.ppermute(x, ("section", "tensor"), both_ways(lambda i, way: (i + way * by) % NT))


def place():
    return lax.axis_index("tensor"), 1 - 2 * lax.rem(lax.axis_index("section"), 2)


def attend_kernel(tiles_ref, q_ref, kv_ref, w_ref, o_ref, q_scr, att_scr, w_scr, sems):
    me, way = place()
    pieces, _, width = w_scr.shape

    def fetch(i):
        columns = pl.ds(pl.multiple_of(i * width, width), width)
        return pltpu.make_async_copy(w_ref.at[:, columns], w_scr.at[i], sems.at[i])

    for i in range(pieces):
        fetch(i).start()

    rows = q_scr.shape[0] // NT
    for p in range(NT):
        start = pl.multiple_of(lax.rem(me + way * p + NT, NT) * rows, rows)
        q_scr[p * rows : (p + 1) * rows, :] = q_ref[pl.ds(start, rows), :]
    group = me // QUAD
    keys = kv_ref[:, pl.ds(pl.multiple_of(group * HD, HD), HD)]
    values = kv_ref[:, pl.ds(pl.multiple_of((KVH + group) * HD, HD), HD)]
    tile = lax.broadcasted_iota(jnp.int32, (1, kv_ref.shape[0]), 1) // TILE_ROWS
    bias = jnp.where(tile < tiles_ref[...], 0.0, -jnp.inf)
    for h in range(q_scr.shape[1] // HD):
        q = q_scr[:, h * HD : (h + 1) * HD]
        s = lax.dot_general(
            q, keys, (((1,), (1,)), ((), ())), preferred_element_type=jnp.float32
        )
        s = s * (1.0 / math.sqrt(HD)) + bias
        e = jnp.exp(s - jnp.max(s, axis=1, keepdims=True))
        p = (e / jnp.sum(e, axis=1, keepdims=True)).astype(jnp.bfloat16)
        att_scr[:, h * HD : (h + 1) * HD] = jnp.dot(
            p, values, preferred_element_type=jnp.float32
        ).astype(jnp.bfloat16)

    @pl.loop(0, pieces)
    def _(i):
        fetch(i).wait()
        columns = pl.ds(pl.multiple_of(i * width, width), width)
        o_ref[:, columns] = jnp.dot(
            att_scr[...], w_scr[i], preferred_element_type=jnp.float32
        ).astype(jnp.bfloat16)


def attend_and_project(tiles, q, kv, weight):
    depth, columns = weight.shape
    width = 1024
    pieces = columns // width
    return pl.pallas_call(
        attend_kernel,
        out_shape=jax.ShapeDtypeStruct((q.shape[0], columns), jnp.bfloat16),
        in_specs=[VMEM, VMEM, VMEM] + [pl.BlockSpec(memory_space=pltpu.HBM)],
        out_specs=VMEM,
        scratch_shapes=[
            pltpu.VMEM(q.shape, jnp.bfloat16),
            pltpu.VMEM(q.shape, jnp.bfloat16),
            pltpu.VMEM((pieces, depth, width), jnp.bfloat16),
            pltpu.SemaphoreType.DMA((pieces,)),
        ],
        compiler_params=pltpu.CompilerParams(vmem_limit_bytes=44 << 20),
        name="attend_and_project",
    )(tiles, q, kv, weight)


def add_rows_kernel(first, sum_ref, part_ref, o_ref):
    rows = sum_ref.shape[0]
    o_ref[...] = (
        sum_ref[...].astype(jnp.float32) + part_ref[first : first + rows, :].astype(jnp.float32)
    ).astype(jnp.bfloat16)


def add_rows(total, projected, block):
    return pl.pallas_call(
        functools.partial(add_rows_kernel, block * total.shape[0]),
        out_shape=jax.ShapeDtypeStruct(total.shape, total.dtype),
        in_specs=[VMEM, VMEM],
        out_specs=VMEM,
        compiler_params=pltpu.CompilerParams(vmem_limit_bytes=8 << 20),
        name="add_rows",
    )(total, projected)


def local(image_tokens, kv_weight, queries, out_weight, residual, gate, tile_counts):
    rows = queries.shape[2] // NT

    tokens = lax.all_gather(image_tokens[0], "section", axis=0, tiled=True)
    partial = jnp.dot(tokens, kv_weight[0], preferred_element_type=jnp.float32)
    keys_values = lax.psum(partial, "tensor").astype(jnp.bfloat16)
    projected = attend_and_project(
        tile_counts.reshape(1, 1), queries[0, 0], keys_values, out_weight[0]
    )

    def part(p):
        return projected[p * rows : (p + 1) * rows]

    up, down = part(8), part(9)
    for k in range(1, 9):
        up = hop(up, 1)
        if k < 8:
            down = hop(down, -1)
            up = add_rows(up, projected, 8 - k)
        if k < 7:
            down = add_rows(down, projected, 9 + k)
    total = up.astype(jnp.float32) + down.astype(jnp.float32) + part(0).astype(jnp.float32)
    mixed = (residual[0, 0].astype(jnp.float32) + jnp.tanh(gate[0]) * total).astype(jnp.bfloat16)
    return mixed[None, None]


def solution(mesh):
    return jax.shard_map(
        local,
        mesh=mesh,
        in_specs=(
            P("dp", "section", "tensor"),
            P("section", "tensor", None),
            P("section", "dp", None, "tensor"),
            P("section", "tensor", None),
            P("section", "dp", "tensor", None),
            P("section"),
            P("dp"),
        ),
        out_specs=P("section", "dp", "tensor", None),
        check_vma=False,
    )
```
